32 devices in a mesh: rep: 4 (over y, x), fsdp: 8 (over z, core).
Axes of the slice: x: 2, y: 2, z: 4, core: 2. Of those that a mesh axis runs over, the one named last changes fastest.
Arguments:
- params: bfloat16 [2, 8192, 4608], P(None, 'fsdp'), may hold values from -6 to 6
- deltas: bfloat16 [4, 2, 8192, 4608], P('rep', None, 'fsdp'), may hold values from -3 to 3
- momentum: float32 [2, 8192, 4608], P(None, 'fsdp', 'rep'), may hold values from -2 to 2
Outputs:
- new_params: bfloat16 [2, 8192, 4608], P(None, 'fsdp')
- new_momentum: float32 [2, 8192, 4608], P(None, 'fsdp', 'rep')
The draws below stay inside these ranges and needn't reach their ends.
All inputs are finite; a program needn't handle non-finite values.
Results may differ from the reference program's by a relative error of at most 0.0035.
Values may be sent and summed in bfloat16 or wider, within the bound.
A program may use at most 192 MiB of HBM per device.

```python
import math
import jax
import jax.numpy as jnp

D = 4608
Q_ROWS = 4096
KV_ROWS = 2048
LAYERS = 2
ROWS = 8192
REPLICAS = 4


def draw_deltas(key, part):
    subkeys = jax.random.split(key, 10)
    row_index = jnp.arange(ROWS, dtype=jnp.int32)
    tensor = (row_index >= Q_ROWS).astype(jnp.int32) + (row_index >= Q_ROWS + KV_ROWS).astype(jnp.int32)
    first_row = jnp.where(tensor == 0, 0, jnp.where(tensor == 1, Q_ROWS, Q_ROWS + KV_ROWS))
    extent = jnp.where(tensor == 0, Q_ROWS, KV_ROWS)
    position = (row_index - first_row).astype(jnp.float32) / extent.astype(jnp.float32)
    amplitude = jnp.exp(jax.random.uniform(subkeys[0], (LAYERS, 3), jnp.float32, math.log(0.1), 0.0))
    replica_amp = jnp.exp(jax.random.uniform(subkeys[1], (REPLICAS, LAYERS, 3), jnp.float32, math.log(0.5), 0.0))
    cycles = jax.random.randint(subkeys[2], (LAYERS, 3), 1, 3).astype(jnp.float32)
    offset = jax.random.uniform(subkeys[9], (LAYERS, 3), jnp.float32, 0.0, 2.0 * math.pi)
    ripple = 0.5 * (1.0 + jnp.sin(2.0 * math.pi * cycles[:, tensor] * position[None, :] + offset[:, tensor]))
    profile = jnp.exp(math.log(0.1) * ripple)
    jitter = jnp.exp(jax.random.uniform(subkeys[4], (LAYERS, ROWS), jnp.float32, math.log(0.5), 0.0))
    columns = jnp.exp(jax.random.uniform(subkeys[5], (LAYERS, D), jnp.float32, math.log(0.1), 0.0))
    signal = jax.random.uniform(subkeys[8], (REPLICAS, LAYERS, ROWS, D), jnp.float32, -1.0, 1.0)
    row_scale = amplitude[:, tensor] * profile * jitter
    values = 3.0 * replica_amp[:, :, tensor][..., None] * row_scale[None, :, :, None] * columns[None, :, None, :] * signal
    return values.astype(jnp.bfloat16)


def levels(stream_key, shape, cuts, low, top_value):
    loudness, own = 1.0, jax.random.fold_in(stream_key, 6)
    for dim, blocks in cuts:
        heights = jnp.exp(jax.random.uniform(jax.random.fold_in(own, dim), (blocks,), jnp.float32, low / len(cuts), top_value / len(cuts)))
        loudness = loudness * jnp.repeat(heights, shape[dim] // blocks).reshape([-1 if axis == dim else 1 for axis in range(len(shape))])
    return loudness


def noise(key, dims, width, most, cuts=(), kind=jnp.bfloat16):
    values = width * jax.random.normal(key, dims, jnp.float32)
    if cuts:
        values = values * levels(key, dims, cuts, -0.22, 0.18)
    return jnp.clip(values, -most, most).astype(kind)


def setup_inputs(seed: int = 0) -> dict:
    seeds = jax.random.split(jax.random.key(seed), 4)
    return {
        "params": noise(seeds[0], (LAYERS, ROWS, D), 1.0, 6.0, ((1, 8),)),
        "deltas": draw_deltas(jax.random.fold_in(seeds[3], 71), 0),
        "momentum": noise(seeds[2], (LAYERS, ROWS, D), 0.3, 2.0, ((1, 8), (2, 4)), jnp.float32),
    }


clip_share = 0.5
peak_eps = 1e-6
outer_rate = 0.7
momentum_decay = 0.9


def reference(params, deltas, momentum):
    row_ids = jnp.arange(ROWS, dtype=jnp.int32)
    tensor_ids = (row_ids >= Q_ROWS).astype(jnp.int32) + (row_ids >= Q_ROWS + KV_ROWS).astype(jnp.int32)
    row_peak = jnp.max(jnp.max(jnp.abs(deltas), axis=3), axis=0).astype(jnp.float32)
    member = tensor_ids[None, :] == jnp.arange(3, dtype=jnp.int32)[:, None]
    peak = jnp.max(jnp.where(member[None], row_peak[:, None, :], jnp.float32(0.0)), axis=2)
    scaled = clip_share * (peak + peak_eps)
    tau = jnp.sum(jnp.where(member[None], scaled[:, :, None], jnp.float32(0.0)), axis=1)
    total = jnp.zeros((LAYERS, ROWS, D), jnp.float32)
    for replica in range(REPLICAS):
        codes = jnp.clip(deltas[replica].astype(jnp.float32) / tau[..., None], -1.0, 1.0).astype(jnp.bfloat16)
        total = total + codes.astype(jnp.float32)
    outer = tau[..., None] * total / jnp.float32(REPLICAS)
    new_momentum = momentum_decay * momentum + outer
    new_params = (params.astype(jnp.float32) - outer_rate * (outer + momentum_decay * new_momentum)).astype(jnp.bfloat16)
    return new_params, new_momentum
```

```python
import functools

import jax
import jax.numpy as jnp
from jax import lax
from jax.experimental import pallas as pl
from jax.experimental.pallas import tpu as pltpu
from jax.sharding import PartitionSpec as P

Q_ROWS = 4096
KV_ROWS = 2048


clip_share = 0.5
peak_eps = 1e-06
outer_rate = 0.7
momentum_decay = 0.9

MESH = pl.DeviceIdType.MESH
CHUNKS_PER_LAYER = 4
EARLY_CHUNKS = 3
STEP_ROWS = 16

Y_OWN, Y_RELAY, X_OWN, X_RELAY = range(4)


def tensor_of(shard, shard_rows):
    row = shard * shard_rows
    return (row >= Q_ROWS).astype(jnp.int32) + (row >= Q_ROWS + KV_ROWS).astype(jnp.int32)


def kernel(
    layers, fsdp, params, deltas, moment, new_params, new_moment,
    local, raw, sum_out, sum_in, fresh, fresh_moment,
    peak, peak_in, group_peak, group_peak_in, tau,
    load_sem, store_sem, raw_send, raw_recv, sum_send, sum_recv,
    own_send, own_recv, relay_send, relay_recv,
    peak_send, peak_recv, group_send, group_recv,
):
    rows, width = moment.shape
    chunks = layers * CHUNKS_PER_LAYER
    chunk = rows // chunks
    half = chunk // 2
    layer_rows = rows // layers
    me = lax.axis_index("rep")
    shard = lax.axis_index("fsdp")
    y, x = me // 2, me % 2
    over_x = y * 2 + (1 - x)
    over_y = (1 - y) * 2 + x
    diagonal = (1 - y) * 2 + (1 - x)
    blocks = (me, over_x, over_y, diagonal)

    def columns(block):
        return pl.ds(pl.multiple_of(block * width, 128), width)

    def whole(c):
        return pl.ds(pl.multiple_of(c * chunk, STEP_ROWS), chunk)

    def first(c):
        return pl.ds(pl.multiple_of(c * chunk, STEP_ROWS), half)

    def second(c):
        return pl.ds(pl.multiple_of(c * chunk + half, STEP_ROWS), half)

    def packed(c):
        return pl.ds(pl.multiple_of(c * half, STEP_ROWS), half)

    def remote(src, dst, send, recv, axis, target):
        return pltpu.make_async_remote_copy(
            src_ref=src, dst_ref=dst, send_sem=send, recv_sem=recv,
            device_id={axis: target}, device_id_type=MESH,
        )

    loads = []
    for layer in range(layers):
        span = pl.ds(layer * layer_rows, layer_rows)
        for slot, block in enumerate(blocks):
            loads.append(
                pltpu.make_async_copy(
                    deltas.at[span, columns(block)], local.at[slot, span], load_sem.at[layer * 4 + slot]
                )
            )
    load_params = pltpu.make_async_copy(params.at[:, columns(me)], fresh, load_sem.at[layers * 4])
    load_moment = pltpu.make_async_copy(moment, fresh_moment, load_sem.at[layers * 4 + 1])
    for load in loads:
        load.start()

    barrier = pltpu.get_barrier_semaphore()
    for step in range(1, fsdp):
        pl.semaphore_signal(
            barrier, inc=1, device_id={"fsdp": lax.rem(shard + step, fsdp)}, device_id_type=MESH
        )
    for block in blocks[1:]:
        pl.semaphore_signal(barrier, inc=1, device_id={"rep": block}, device_id_type=MESH)
    pl.semaphore_wait(barrier, fsdp - 1 + 3)

    def raw_copy(kind, c):
        target = over_y if kind in (Y_OWN, Y_RELAY) else over_x
        span = first(c) if kind in (Y_OWN, Y_RELAY) else second(c)
        block = diagonal if kind in (Y_RELAY, X_RELAY) else target
        return remote(
            deltas.at[span, columns(block)], raw.at[kind, packed(c)],
            raw_send.at[kind, c], raw_recv.at[kind, c], "rep", target,
        )

    def sum_copy(link, c):
        return remote(
            sum_out.at[link, packed(c)], sum_in.at[link, packed(c)],
            sum_send.at[link, c], sum_recv.at[link, c], "rep", over_x if link == 0 else over_y,
        )

    def own_copy(link, c):
        return remote(
            fresh.at[whole(c)], new_params.at[whole(c), columns(me)],
            own_send.at[link, c], own_recv.at[link, c], "rep", over_x if link == 0 else over_y,
        )

    def relay_copy(link, c):
        piece = (second(c), columns(over_y)) if link == 0 else (first(c), columns(over_x))
        return remote(
            new_params.at[piece], new_params.at[piece],
            relay_send.at[link, c], relay_recv.at[link, c], "rep", over_x if link == 0 else over_y,
        )

    def start_raw(c, carry):
        for kind in (Y_RELAY, X_RELAY, Y_OWN, X_OWN):
            raw_copy(kind, c).start()
        return carry

    lax.fori_loop(0, EARLY_CHUNKS, start_raw, 0)

    for layer in range(layers):
        for slot in range(4):
            loads[layer * 4 + slot].wait()

        def largest(i, top):
            span = pl.ds(pl.multiple_of(layer * layer_rows + i * STEP_ROWS, STEP_ROWS), STEP_ROWS)
            for slot in range(4):
                top = jnp.maximum(top, jnp.abs(local[slot, span, :]))
            return top

        top = lax.fori_loop(
            0, layer_rows // STEP_ROWS, largest, jnp.zeros((STEP_ROWS, width), local.dtype)
        ).astype(jnp.float32)
        top = functools.reduce(
            jnp.maximum, [top[:, k * 128 : (k + 1) * 128] for k in range(width // 128)]
        )
        peak[layer] = jnp.maximum(top[:8], top[8:])

    def peak_copy(step):
        return remote(
            peak, peak_in.at[step - 1], peak_send.at[step - 1], peak_recv.at[step - 1],
            "fsdp", lax.rem(shard + step, fsdp),
        )

    for step in range(1, fsdp):
        peak_copy(step).start()
    load_params.start()
    load_moment.start()
    mine = tensor_of(shard, layer_rows)
    for layer in range(layers):
        group_peak[layer] = peak[layer]
    for step in range(1, fsdp):
        peak_copy(step).wait_recv()
        same = tensor_of(lax.rem(shard + fsdp - step, fsdp), layer_rows) == mine
        share = jnp.where(same, jnp.float32(1.0), jnp.float32(0.0))
        for layer in range(layers):
            group_peak[layer] = jnp.maximum(group_peak[layer], peak_in[step - 1, layer] * share)

    def group_copy(slot):
        return remote(
            group_peak, group_peak_in.at[slot], group_send.at[slot], group_recv.at[slot],
            "rep", blocks[slot + 1],
        )

    for slot in range(3):
        group_copy(slot).start()
    lax.fori_loop(EARLY_CHUNKS, chunks, start_raw, 0)
    for slot in range(3):
        group_copy(slot).wait_recv()
    for layer in range(layers):
        top = group_peak[layer]
        for slot in range(3):
            top = jnp.maximum(top, group_peak_in[slot, layer])
        top = jnp.max(jnp.max(top, axis=0, keepdims=True), axis=1, keepdims=True)
        tau[layer] = jnp.broadcast_to(clip_share * (top + peak_eps), tau.shape[1:])

    def code(values, scale):
        return jnp.clip(values.astype(jnp.float32) / scale, -1.0, 1.0).astype(jnp.bfloat16).astype(jnp.float32)

    def relay_sums(c, carry):
        layer = c // CHUNKS_PER_LAYER
        for link, kind in ((0, Y_RELAY), (1, X_RELAY)):
            raw_copy(kind, c).wait_recv()
            start = c * chunk + link * half

            def add(i, inner):
                here = pl.ds(pl.multiple_of(start + i * STEP_ROWS, STEP_ROWS), STEP_ROWS)
                there = pl.ds(pl.multiple_of(c * half + i * STEP_ROWS, STEP_ROWS), STEP_ROWS)
                scale = tau[layer]
                total = code(local[1 + link, here, :], scale) + code(raw[kind, there, :], scale)
                sum_out[link, there, :] = total.astype(jnp.bfloat16)
                return inner

            lax.fori_loop(0, half // STEP_ROWS, add, 0)
            sum_copy(link, c).start()
        return carry

    lax.fori_loop(0, chunks, relay_sums, 0)

    load_params.wait()
    load_moment.wait()

    def store_params(c):
        return pltpu.make_async_copy(
            fresh.at[whole(c)], new_params.at[whole(c), columns(me)], store_sem.at[0, c]
        )

    def store_moment(c):
        return pltpu.make_async_copy(
            fresh_moment.at[whole(c)], new_moment.at[whole(c)], store_sem.at[1, c]
        )

    def update(c, carry):
        layer = c // CHUNKS_PER_LAYER
        for link, kind in ((0, Y_OWN), (1, X_OWN)):
            raw_copy(kind, c).wait_recv()
            sum_copy(link, c).wait_recv()
            start = c * chunk + link * half

            def apply(i, inner):
                here = pl.ds(pl.multiple_of(start + i * STEP_ROWS, STEP_ROWS), STEP_ROWS)
                there = pl.ds(pl.multiple_of(c * half + i * STEP_ROWS, STEP_ROWS), STEP_ROWS)
                scale = tau[layer]
                total = code(local[0, here, :], scale) + code(raw[kind, there, :], scale)
                total = total + sum_in[link, there, :].astype(jnp.float32)
                outer = scale * total / jnp.float32(4)
                moved = momentum_decay * fresh_moment[here, :] + outer
                fresh_moment[here, :] = moved
                fresh[here, :] = (
                    fresh[here, :].astype(jnp.float32) - outer_rate * (outer + momentum_decay * moved)
                ).astype(jnp.bfloat16)
                return inner

            lax.fori_loop(0, half // STEP_ROWS, apply, 0)
        own_copy(0, c).start()
        own_copy(1, c).start()
        store_params(c).start()
        store_moment(c).start()
        return carry

    lax.fori_loop(0, chunks, update, 0)

    def relay(c, carry):
        own_copy(0, c).wait_recv()
        relay_copy(1, c).start()
        own_copy(1, c).wait_recv()
        relay_copy(0, c).start()
        return carry

    lax.fori_loop(0, chunks, relay, 0)

    def drain(c, carry):
        for kind in range(4):
            raw_copy(kind, c).wait_send()
        store_params(c).wait()
        store_moment(c).wait()
        for link in range(2):
            sum_copy(link, c).wait_send()
            own_copy(link, c).wait_send()
            relay_copy(link, c).wait()
        return carry

    for step in range(1, fsdp):
        peak_copy(step).wait_send()
    for slot in range(3):
        group_copy(slot).wait_send()
    lax.fori_loop(0, chunks, drain, 0)


def on_device(rep, fsdp, params, deltas, momentum):
    layers, shard_rows, depth = params.shape
    width = momentum.shape[2]
    rows = layers * shard_rows
    chunks = layers * CHUNKS_PER_LAYER
    assert rep == 4 and width * rep == depth and width % 128 == 0
    assert Q_ROWS % shard_rows == 0 and KV_ROWS % shard_rows == 0
    assert shard_rows % (CHUNKS_PER_LAYER * 2 * STEP_ROWS) == 0
    dma = pltpu.SemaphoreType.DMA
    hbm = pl.BlockSpec(memory_space=pl.ANY)
    new_params, new_momentum = pl.pallas_call(
        functools.partial(kernel, layers, fsdp),
        out_shape=(
            jax.ShapeDtypeStruct((rows, depth), params.dtype),
            jax.ShapeDtypeStruct((rows, width), momentum.dtype),
        ),
        in_specs=[hbm] * 3,
        out_specs=(hbm, hbm),
        scratch_shapes=[
            pltpu.VMEM((4, rows, width), deltas.dtype),
            pltpu.VMEM((4, rows // 2, width), deltas.dtype),
            pltpu.VMEM((2, rows // 2, width), jnp.bfloat16),
            pltpu.VMEM((2, rows // 2, width), jnp.bfloat16),
            pltpu.VMEM((rows, width), params.dtype),
            pltpu.VMEM((rows, width), momentum.dtype),
            pltpu.VMEM((layers, 8, 128), jnp.float32),
            pltpu.VMEM((fsdp - 1, layers, 8, 128), jnp.float32),
            pltpu.VMEM((layers, 8, 128), jnp.float32),
            pltpu.VMEM((3, layers, 8, 128), jnp.float32),
            pltpu.VMEM((layers, STEP_ROWS, width), jnp.float32),
            dma((layers * 4 + 2,)),
            dma((2, chunks)),
            dma((4, chunks)),
            dma((4, chunks)),
            dma((2, chunks)),
            dma((2, chunks)),
            dma((2, chunks)),
            dma((2, chunks)),
            dma((2, chunks)),
            dma((2, chunks)),
            dma((fsdp - 1,)),
            dma((fsdp - 1,)),
            dma((3,)),
            dma((3,)),
        ],
        compiler_params=pltpu.CompilerParams(
            collective_id=0, has_side_effects=True, vmem_limit_bytes=60 * 1024 * 1024
        ),
        name="outer_step",
    )(
        params.reshape(rows, depth),
        deltas.reshape(rows, depth),
        momentum.reshape(rows, width),
    )
    return (
        new_params.reshape(params.shape),
        new_momentum.reshape(momentum.shape),
    )


def solution(mesh):
    placed = (P(None, "fsdp", None), P("rep", None, "fsdp", None), P(None, "fsdp", "rep"))
    return jax.shard_map(
        functools.partial(on_device, mesh.shape["rep"], mesh.shape["fsdp"]),
        mesh=mesh,
        in_specs=placed,
        out_specs=(P(None, "fsdp", None), P(None, "fsdp", "rep")),
        check_vma=False,
    )
```

```python
import functools

import jax
import jax.numpy as jnp
from jax import lax
from jax.experimental import pallas as pl
from jax.experimental.pallas import tpu as pltpu
from jax.sharding import PartitionSpec as P

Q_ROWS = 4096
KV_ROWS = 2048


clip_share = 0.5
peak_eps = 1e-06
outer_rate = 0.7
momentum_decay = 0.9

MESH = pl.DeviceIdType.MESH
CHUNKS_PER_LAYER = 4
EARLY_CHUNKS = 3
STEP_ROWS = 16

Y_OWN, Y_RELAY, X_OWN, X_RELAY = range(4)


def tensor_of(shard, shard_rows):
    row = shard * shard_rows
    return (row >= Q_ROWS).astype(jnp.int32) + (row >= Q_ROWS + KV_ROWS).astype(jnp.int32)


def kernel(
    layers, fsdp, params, deltas, moment, new_params, new_moment,
    local, raw, sum_out, sum_in,
    peak, peak_in, group_peak, group_peak_in, tau,
    load_sem, raw_send, raw_recv, sum_send, sum_recv,
    own_send, own_recv, relay_send, relay_recv,
    peak_send, peak_recv, group_send, group_recv,
):
    rows, width = moment.shape
    chunks = layers * CHUNKS_PER_LAYER
    chunk = rows // chunks
    half = chunk // 2
    layer_rows = rows // layers
    me = lax.axis_index("rep")
    shard = lax.axis_index("fsdp")
    y, x = me // 2, me % 2
    over_x = y * 2 + (1 - x)
    over_y = (1 - y) * 2 + x
    diagonal = (1 - y) * 2 + (1 - x)
    blocks = (me, over_x, over_y, diagonal)

    def columns(block):
        return pl.ds(pl.multiple_of(block * width, 128), width)

    def whole(c):
        return pl.ds(pl.multiple_of(c * chunk, STEP_ROWS), chunk)

    def first(c):
        return pl.ds(pl.multiple_of(c * chunk, STEP_ROWS), half)

    def second(c):
        return pl.ds(pl.multiple_of(c * chunk + half, STEP_ROWS), half)

    def packed(c):
        return pl.ds(pl.multiple_of(c * half, STEP_ROWS), half)

    def remote(src, dst, send, recv, axis, target):
        return pltpu.make_async_remote_copy(
            src_ref=src, dst_ref=dst, send_sem=send, recv_sem=recv,
            device_id={axis: target}, device_id_type=MESH,
        )

    loads = []
    for layer in range(layers):
        span = pl.ds(layer * layer_rows, layer_rows)
        for slot, block in enumerate(blocks):
            loads.append(
                pltpu.make_async_copy(
                    deltas.at[span, columns(block)],
                    local.at[slot, span] if slot < 3 else new_params.at[diagonal, span],
                    load_sem.at[layer * 4 + slot],
                )
            )
    load_params = pltpu.make_async_copy(params.at[:, columns(me)], new_params.at[me], load_sem.at[layers * 4])
    load_moment = pltpu.make_async_copy(moment, new_moment, load_sem.at[layers * 4 + 1])
    for load in loads:
        load.start()

    barrier = pltpu.get_barrier_semaphore()
    for step in range(1, fsdp):
        pl.semaphore_signal(
            barrier, inc=1, device_id={"fsdp": lax.rem(shard + step, fsdp)}, device_id_type=MESH
        )
    for block in blocks[1:]:
        pl.semaphore_signal(barrier, inc=1, device_id={"rep": block}, device_id_type=MESH)
    pl.semaphore_wait(barrier, fsdp - 1 + 3)

    def raw_copy(kind, c):
        target = over_y if kind in (Y_OWN, Y_RELAY) else over_x
        span = first(c) if kind in (Y_OWN, Y_RELAY) else second(c)
        block = diagonal if kind in (Y_RELAY, X_RELAY) else target
        return remote(
            deltas.at[span, columns(block)], raw.at[kind, packed(c)],
            raw_send.at[kind, c], raw_recv.at[kind, c], "rep", target,
        )

    def sum_copy(link, c):
        return remote(
            sum_out.at[link, packed(c)], sum_in.at[link, packed(c)],
            sum_send.at[link, c], sum_recv.at[link, c], "rep", over_x if link == 0 else over_y,
        )

    def own_copy(link, c):
        return remote(
            new_params.at[me, whole(c)], new_params.at[me, whole(c)],
            own_send.at[link, c], own_recv.at[link, c], "rep", over_x if link == 0 else over_y,
        )

    def relay_copy(link, c):
        piece = (over_y, second(c)) if link == 0 else (over_x, first(c))
        return remote(
            new_params.at[piece], new_params.at[piece],
            relay_send.at[link, c], relay_recv.at[link, c], "rep", over_x if link == 0 else over_y,
        )

    def start_raw(c, carry):
        for kind in (Y_RELAY, X_RELAY, Y_OWN, X_OWN):
            raw_copy(kind, c).start()
        return carry

    lax.fori_loop(0, EARLY_CHUNKS, start_raw, 0)

    for layer in range(layers):
        for slot in range(4):
            loads[layer * 4 + slot].wait()

        def largest(i, top):
            span = pl.ds(pl.multiple_of(layer * layer_rows + i * STEP_ROWS, STEP_ROWS), STEP_ROWS)
            for slot in range(3):
                top = jnp.maximum(top, jnp.abs(local[slot, span, :]))
            return jnp.maximum(top, jnp.abs(new_params[diagonal, span, :]))

        top = lax.fori_loop(
            0, layer_rows // STEP_ROWS, largest, jnp.zeros((STEP_ROWS, width), local.dtype)
        ).astype(jnp.float32)
        top = functools.reduce(
            jnp.maximum, [top[:, k * 128 : (k + 1) * 128] for k in range(width // 128)]
        )
        peak[layer] = jnp.maximum(top[:8], top[8:])

    def peak_copy(step):
        return remote(
            peak, peak_in.at[step - 1], peak_send.at[step - 1], peak_recv.at[step - 1],
            "fsdp", lax.rem(shard + step, fsdp),
        )

    for step in range(1, fsdp):
        peak_copy(step).start()
    load_params.start()
    load_moment.start()
    mine = tensor_of(shard, layer_rows)
    for layer in range(layers):
        group_peak[layer] = peak[layer]
    for step in range(1, fsdp):
        peak_copy(step).wait_recv()
        same = tensor_of(lax.rem(shard + fsdp - step, fsdp), layer_rows) == mine
        share = jnp.where(same, jnp.float32(1.0), jnp.float32(0.0))
        for layer in range(layers):
            group_peak[layer] = jnp.maximum(group_peak[layer], peak_in[step - 1, layer] * share)

    def group_copy(slot):
        return remote(
            group_peak, group_peak_in.at[slot], group_send.at[slot], group_recv.at[slot],
            "rep", blocks[slot + 1],
        )

    for slot in range(3):
        group_copy(slot).start()
    lax.fori_loop(EARLY_CHUNKS, chunks, start_raw, 0)
    for slot in range(3):
        group_copy(slot).wait_recv()
    for layer in range(layers):
        top = group_peak[layer]
        for slot in range(3):
            top = jnp.maximum(top, group_peak_in[slot, layer])
        top = jnp.max(jnp.max(top, axis=0, keepdims=True), axis=1, keepdims=True)
        tau[layer] = jnp.broadcast_to(clip_share * (top + peak_eps), tau.shape[1:])

    def code(values, scale):
        return jnp.clip(values.astype(jnp.float32) / scale, -1.0, 1.0).astype(jnp.bfloat16).astype(jnp.float32)

    def relay_sums(c, carry):
        layer = c // CHUNKS_PER_LAYER
        for link, kind in ((0, Y_RELAY), (1, X_RELAY)):
            raw_copy(kind, c).wait_recv()
            start = c * chunk + link * half

            def add(i, inner):
                here = pl.ds(pl.multiple_of(start + i * STEP_ROWS, STEP_ROWS), STEP_ROWS)
                there = pl.ds(pl.multiple_of(c * half + i * STEP_ROWS, STEP_ROWS), STEP_ROWS)
                scale = tau[layer]
                total = code(local[1 + link, here, :], scale) + code(raw[kind, there, :], scale)
                sum_out[link, there, :] = total.astype(jnp.bfloat16)
                return inner

            lax.fori_loop(0, half // STEP_ROWS, add, 0)
            sum_copy(link, c).start()
        return carry

    lax.fori_loop(0, chunks, relay_sums, 0)

    load_params.wait()
    load_moment.wait()

    def update(c, carry):
        layer = c // CHUNKS_PER_LAYER
        for link, kind in ((0, Y_OWN), (1, X_OWN)):
            raw_copy(kind, c).wait_recv()
            sum_copy(link, c).wait_recv()
            start = c * chunk + link * half

            def apply(i, inner):
                here = pl.ds(pl.multiple_of(start + i * STEP_ROWS, STEP_ROWS), STEP_ROWS)
                there = pl.ds(pl.multiple_of(c * half + i * STEP_ROWS, STEP_ROWS), STEP_ROWS)
                scale = tau[layer]
                total = code(local[0, here, :], scale) + code(raw[kind, there, :], scale)
                total = total + sum_in[link, there, :].astype(jnp.float32)
                outer = scale * total / jnp.float32(4)
                moved = momentum_decay * new_moment[here, :] + outer
                new_moment[here, :] = moved
                new_params[me, here, :] = (
                    new_params[me, here, :].astype(jnp.float32) - outer_rate * (outer + momentum_decay * moved)
                ).astype(jnp.bfloat16)
                return inner

            lax.fori_loop(0, half // STEP_ROWS, apply, 0)
        own_copy(0, c).start()
        own_copy(1, c).start()
        return carry

    lax.fori_loop(0, chunks, update, 0)

    def relay(c, carry):
        own_copy(0, c).wait_recv()
        relay_copy(1, c).start()
        own_copy(1, c).wait_recv()
        relay_copy(0, c).start()
        return carry

    lax.fori_loop(0, chunks, relay, 0)

    def drain(c, carry):
        for kind in range(4):
            raw_copy(kind, c).wait_send()
        for link in range(2):
            sum_copy(link, c).wait_send()
            own_copy(link, c).wait_send()
            relay_copy(link, c).wait()
        return carry

    for step in range(1, fsdp):
        peak_copy(step).wait_send()
    for slot in range(3):
        group_copy(slot).wait_send()
    lax.fori_loop(0, chunks, drain, 0)


def store_outputs(blocks, fresh_moment, new_params, new_moment, sems):
    count, _, width = blocks.shape
    stores = [
        pltpu.make_async_copy(blocks.at[k], new_params.at[:, pl.ds(k * width, width)], sems.at[k])
        for k in range(count)
    ]
    stores.append(pltpu.make_async_copy(fresh_moment, new_moment, sems.at[count]))
    for store in stores:
        store.start()
    for store in stores:
        store.wait()


def on_device(rep, fsdp, params, deltas, momentum):
    layers, shard_rows, depth = params.shape
    width = momentum.shape[2]
    rows = layers * shard_rows
    chunks = layers * CHUNKS_PER_LAYER
    assert rep == 4 and width * rep == depth and width % 128 == 0
    assert Q_ROWS % shard_rows == 0 and KV_ROWS % shard_rows == 0
    assert shard_rows % (CHUNKS_PER_LAYER * 2 * STEP_ROWS) == 0
    block_bytes = rows * width * 2
    kernel_bytes = block_bytes * 7 + (2 << 20)
    dma = pltpu.SemaphoreType.DMA
    hbm = pl.BlockSpec(memory_space=pl.ANY)
    vmem = pl.BlockSpec(memory_space=pltpu.VMEM)
    blocks, fresh_moment = pl.pallas_call(
        functools.partial(kernel, layers, fsdp),
        out_shape=(
            pltpu.VMEM((rep, rows, width), params.dtype),
            pltpu.VMEM((rows, width), momentum.dtype),
        ),
        in_specs=[hbm] * 3,
        out_specs=(vmem, vmem),
        scratch_shapes=[
            pltpu.VMEM((3, rows, width), deltas.dtype),
            pltpu.VMEM((4, rows // 2, width), deltas.dtype),
            pltpu.VMEM((2, rows // 2, width), jnp.bfloat16),
            pltpu.VMEM((2, rows // 2, width), jnp.bfloat16),
            pltpu.VMEM((layers, 8, 128), jnp.float32),
            pltpu.VMEM((fsdp - 1, layers, 8, 128), jnp.float32),
            pltpu.VMEM((layers, 8, 128), jnp.float32),
            pltpu.VMEM((3, layers, 8, 128), jnp.float32),
            pltpu.VMEM((layers, STEP_ROWS, width), jnp.float32),
            dma((layers * 4 + 2,)),
            dma((4, chunks)),
            dma((4, chunks)),
            dma((2, chunks)),
            dma((2, chunks)),
            dma((2, chunks)),
            dma((2, chunks)),
            dma((2, chunks)),
            dma((2, chunks)),
            dma((fsdp - 1,)),
            dma((fsdp - 1,)),
            dma((3,)),
            dma((3,)),
        ],
        compiler_params=pltpu.CompilerParams(
            collective_id=0, has_side_effects=True, vmem_limit_bytes=kernel_bytes
        ),
        name="outer_step",
    )(
        params.reshape(rows, depth),
        deltas.reshape(rows, depth),
        momentum.reshape(rows, width),
    )
    new_params, new_momentum = pl.pallas_call(
        store_outputs,
        out_shape=(
            jax.ShapeDtypeStruct((rows, depth), params.dtype),
            jax.ShapeDtypeStruct((rows, width), momentum.dtype),
        ),
        in_specs=[vmem] * 2,
        out_specs=(hbm, hbm),
        scratch_shapes=[dma((rep + 1,))],
        compiler_params=pltpu.CompilerParams(vmem_limit_bytes=1 << 20),
        name="store_outputs",
    )(
        pltpu.with_memory_space_constraint(blocks, pltpu.VMEM),
        pltpu.with_memory_space_constraint(fresh_moment, pltpu.VMEM),
    )
    return (
        new_params.reshape(params.shape),
        new_momentum.reshape(momentum.shape),
    )


def solution(mesh):
    placed = (P(None, "fsdp", None), P("rep", None, "fsdp", None), P(None, "fsdp", "rep"))
    return jax.shard_map(
        functools.partial(on_device, mesh.shape["rep"], mesh.shape["fsdp"]),
        mesh=mesh,
        in_specs=placed,
        out_specs=(P(None, "fsdp", None), P(None, "fsdp", "rep")),
        check_vma=False,
    )
```

```python
import functools

import jax
import jax.numpy as jnp
from jax import lax
from jax.experimental import pallas as pl
from jax.experimental.pallas import tpu as pltpu
from jax.sharding import PartitionSpec as P

Q_ROWS = 4096
KV_ROWS = 2048


clip_share = 0.5
peak_eps = 1e-06
outer_rate = 0.7
momentum_decay = 0.9

MESH = pl.DeviceIdType.MESH
CHUNKS_PER_LAYER = 4
EARLY_CHUNKS = 2
STEP_ROWS = 16

Y_OWN, Y_RELAY, X_OWN, X_RELAY = range(4)


def tensor_of(shard, shard_rows):
    row = shard * shard_rows
    return (row >= Q_ROWS).astype(jnp.int32) + (row >= Q_ROWS + KV_ROWS).astype(jnp.int32)


def kernel(
    layers, fsdp, params, deltas, moment, new_params, new_moment,
    local, raw, sum_out, sum_in,
    peak, group_peak, group_peak_in, run_peak, run_peak_in, tau,
    load_sem, raw_send, raw_recv, sum_send, sum_recv,
    own_send, own_recv, relay_send, relay_recv,
    group_send, group_recv, run_send, run_recv,
):
    rows, width = moment.shape
    chunks = layers * CHUNKS_PER_LAYER
    chunk = rows // chunks
    half = chunk // 2
    layer_rows = rows // layers
    me = lax.axis_index("rep")
    shard = lax.axis_index("fsdp")
    y, x = me // 2, me % 2
    over_x = y * 2 + (1 - x)
    over_y = (1 - y) * 2 + x
    diagonal = (1 - y) * 2 + (1 - x)
    blocks = (me, over_x, over_y, diagonal)

    def columns(block):
        return pl.ds(pl.multiple_of(block * width, 128), width)

    def whole(c):
        return pl.ds(pl.multiple_of(c * chunk, STEP_ROWS), chunk)

    def first(c):
        return pl.ds(pl.multiple_of(c * chunk, STEP_ROWS), half)

    def second(c):
        return pl.ds(pl.multiple_of(c * chunk + half, STEP_ROWS), half)

    def packed(c):
        return pl.ds(pl.multiple_of(c * half, STEP_ROWS), half)

    def remote(src, dst, send, recv, axis, target):
        return pltpu.make_async_remote_copy(
            src_ref=src, dst_ref=dst, send_sem=send, recv_sem=recv,
            device_id={axis: target}, device_id_type=MESH,
        )

    loads = []
    for layer in range(layers):
        span = pl.ds(layer * layer_rows, layer_rows)
        for slot, block in enumerate(blocks):
            loads.append(
                pltpu.make_async_copy(
                    deltas.at[span, columns(block)],
                    local.at[slot, span] if slot < 3 else new_params.at[diagonal, span],
                    load_sem.at[layer * 4 + slot],
                )
            )
    load_params = pltpu.make_async_copy(params.at[:, columns(me)], new_params.at[me], load_sem.at[layers * 4])
    load_moment = pltpu.make_async_copy(moment, new_moment, load_sem.at[layers * 4 + 1])
    for load in loads:
        load.start()

    barrier = pltpu.get_barrier_semaphore()
    for target in (over_x, over_y):
        pl.semaphore_signal(barrier, inc=1, device_id={"rep": target}, device_id_type=MESH)

    @pl.when(shard > 0)
    def _():
        pl.semaphore_signal(barrier, inc=1, device_id={"fsdp": shard - 1}, device_id_type=MESH)

    @pl.when(shard < fsdp - 1)
    def _():
        pl.semaphore_signal(barrier, inc=1, device_id={"fsdp": shard + 1}, device_id_type=MESH)

    inner = jnp.where(shard > 0, 1, 0) + jnp.where(shard < fsdp - 1, 1, 0)
    pl.semaphore_wait(barrier, 2 + inner)

    def raw_copy(kind, c):
        target = over_y if kind in (Y_OWN, Y_RELAY) else over_x
        span = first(c) if kind in (Y_OWN, Y_RELAY) else second(c)
        block = diagonal if kind in (Y_RELAY, X_RELAY) else target
        return remote(
            deltas.at[span, columns(block)], raw.at[kind, packed(c)],
            raw_send.at[kind, c], raw_recv.at[kind, c], "rep", target,
        )

    def sum_copy(link, c):
        return remote(
            sum_out.at[link, packed(c)], sum_in.at[link, packed(c)],
            sum_send.at[link, c], sum_recv.at[link, c], "rep", over_x if link == 0 else over_y,
        )

    def own_copy(link, c):
        return remote(
            new_params.at[me, whole(c)], new_params.at[me, whole(c)],
            own_send.at[link, c], own_recv.at[link, c], "rep", over_x if link == 0 else over_y,
        )

    def relay_copy(link, c):
        piece = (over_y, second(c)) if link == 0 else (over_x, first(c))
        return remote(
            new_params.at[piece], new_params.at[piece],
            relay_send.at[link, c], relay_recv.at[link, c], "rep", over_x if link == 0 else over_y,
        )

    def start_raw(c, carry):
        for kind in (Y_RELAY, X_RELAY, Y_OWN, X_OWN):
            raw_copy(kind, c).start()
        return carry

    lax.fori_loop(0, EARLY_CHUNKS, start_raw, 0)

    for layer in range(layers):
        for slot in range(4):
            loads[layer * 4 + slot].wait()

        def largest(i, top):
            span = pl.ds(pl.multiple_of(layer * layer_rows + i * STEP_ROWS, STEP_ROWS), STEP_ROWS)
            for slot in range(3):
                top = jnp.maximum(top, jnp.abs(local[slot, span, :]))
            return jnp.maximum(top, jnp.abs(new_params[diagonal, span, :]))

        top = lax.fori_loop(
            0, layer_rows // STEP_ROWS, largest, jnp.zeros((STEP_ROWS, width), local.dtype)
        ).astype(jnp.float32)
        top = functools.reduce(
            jnp.maximum, [top[:, k * 128 : (k + 1) * 128] for k in range(width // 128)]
        )
        peak[layer] = jnp.maximum(top[:8], top[8:])

    load_params.start()
    load_moment.start()

    def group_copy(step):
        return remote(
            peak if step == 0 else group_peak, group_peak_in.at[step],
            group_send.at[step], group_recv.at[step], "rep", over_x if step == 0 else over_y,
        )

    group_copy(0).start()
    lax.fori_loop(EARLY_CHUNKS, EARLY_CHUNKS + 1, start_raw, 0)
    group_copy(0).wait_recv()
    group_peak[...] = jnp.maximum(peak[...], group_peak_in[0])
    group_copy(1).start()
    lax.fori_loop(EARLY_CHUNKS + 1, chunks, start_raw, 0)
    group_copy(1).wait_recv()
    for way in range(2):
        run_peak[way] = jnp.maximum(group_peak[...], group_peak_in[1])

    def line_copy(way):
        return remote(
            run_peak.at[way], run_peak_in.at[way], run_send.at[way], run_recv.at[way],
            "fsdp", shard + 1 if way == 0 else shard - 1,
        )

    mine = tensor_of(shard, layer_rows)
    has_left, has_right = shard > 0, shard < fsdp - 1
    for way, behind, ahead, before in (
        (0, has_left, has_right, shard - 1),
        (1, has_right, has_left, shard + 1),
    ):
        share = jnp.where(tensor_of(before, layer_rows) == mine, jnp.float32(1.0), jnp.float32(0.0))

        @pl.when(behind)
        def _():
            line_copy(way).wait_recv()
            run_peak[way] = jnp.maximum(run_peak[way], run_peak_in[way] * share)

        @pl.when(ahead)
        def _():
            line_copy(way).start()

    for layer in range(layers):
        top = jnp.maximum(run_peak[0, layer], run_peak[1, layer])
        top = jnp.max(jnp.max(top, axis=0, keepdims=True), axis=1, keepdims=True)
        tau[layer] = jnp.broadcast_to(clip_share * (top + peak_eps), tau.shape[1:])

    def code(values, scale):
        return jnp.clip(values.astype(jnp.float32) / scale, -1.0, 1.0).astype(jnp.bfloat16).astype(jnp.float32)

    def relay_sums(c, carry):
        layer = c // CHUNKS_PER_LAYER
        for link, kind in ((0, Y_RELAY), (1, X_RELAY)):
            raw_copy(kind, c).wait_recv()
            start = c * chunk + link * half

            def add(i, inner):
                here = pl.ds(pl.multiple_of(start + i * STEP_ROWS, STEP_ROWS), STEP_ROWS)
                there = pl.ds(pl.multiple_of(c * half + i * STEP_ROWS, STEP_ROWS), STEP_ROWS)
                scale = tau[layer]
                total = code(local[1 + link, here, :], scale) + code(raw[kind, there, :], scale)
                sum_out[link, there, :] = total.astype(jnp.bfloat16)
                return inner

            lax.fori_loop(0, half // STEP_ROWS, add, 0)
            sum_copy(link, c).start()
        return carry

    lax.fori_loop(0, chunks, relay_sums, 0)

    load_params.wait()
    load_moment.wait()

    def update(c, carry):
        layer = c // CHUNKS_PER_LAYER
        for link, kind in ((0, Y_OWN), (1, X_OWN)):
            raw_copy(kind, c).wait_recv()
            sum_copy(link, c).wait_recv()
            start = c * chunk + link * half

            def apply(i, inner):
                here = pl.ds(pl.multiple_of(start + i * STEP_ROWS, STEP_ROWS), STEP_ROWS)
                there = pl.ds(pl.multiple_of(c * half + i * STEP_ROWS, STEP_ROWS), STEP_ROWS)
                scale = tau[layer]
                total = code(local[0, here, :], scale) + code(raw[kind, there, :], scale)
                total = total + sum_in[link, there, :].astype(jnp.float32)
                outer = scale * total / jnp.float32(4)
                moved = momentum_decay * new_moment[here, :] + outer
                new_moment[here, :] = moved
                new_params[me, here, :] = (
                    new_params[me, here, :].astype(jnp.float32) - outer_rate * (outer + momentum_decay * moved)
                ).astype(jnp.bfloat16)
                return inner

            lax.fori_loop(0, half // STEP_ROWS, apply, 0)
        own_copy(0, c).start()
        own_copy(1, c).start()
        return carry

    lax.fori_loop(0, chunks, update, 0)

    def relay(c, carry):
        own_copy(0, c).wait_recv()
        relay_copy(1, c).start()
        own_copy(1, c).wait_recv()
        relay_copy(0, c).start()
        return carry

    lax.fori_loop(0, chunks, relay, 0)

    def drain(c, carry):
        for kind in range(4):
            raw_copy(kind, c).wait_send()
        for link in range(2):
            sum_copy(link, c).wait_send()
            own_copy(link, c).wait_send()
            relay_copy(link, c).wait()
        return carry

    for way, ahead in ((0, has_right), (1, has_left)):

        @pl.when(ahead)
        def _():
            line_copy(way).wait_send()

    for step in range(2):
        group_copy(step).wait_send()
    lax.fori_loop(0, chunks, drain, 0)


def store_outputs(blocks, fresh_moment, new_params, new_moment, sems):
    count, _, width = blocks.shape
    stores = [
        pltpu.make_async_copy(blocks.at[k], new_params.at[:, pl.ds(k * width, width)], sems.at[k])
        for k in range(count)
    ]
    stores.append(pltpu.make_async_copy(fresh_moment, new_moment, sems.at[count]))
    for store in stores:
        store.start()
    for store in stores:
        store.wait()


def on_device(rep, fsdp, params, deltas, momentum):
    layers, shard_rows, depth = params.shape
    width = momentum.shape[2]
    rows = layers * shard_rows
    chunks = layers * CHUNKS_PER_LAYER
    assert rep == 4 and width * rep == depth and width % 128 == 0
    assert Q_ROWS % shard_rows == 0 and KV_ROWS % shard_rows == 0
    assert shard_rows % (CHUNKS_PER_LAYER * 2 * STEP_ROWS) == 0
    block_bytes = rows * width * 2
    kernel_bytes = block_bytes * 7 + (2 << 20)
    dma = pltpu.SemaphoreType.DMA
    hbm = pl.BlockSpec(memory_space=pl.ANY)
    vmem = pl.BlockSpec(memory_space=pltpu.VMEM)
    blocks, fresh_moment = pl.pallas_call(
        functools.partial(kernel, layers, fsdp),
        out_shape=(
            pltpu.VMEM((rep, rows, width), params.dtype),
            pltpu.VMEM((rows, width), momentum.dtype),
        ),
        in_specs=[hbm] * 3,
        out_specs=(vmem, vmem),
        scratch_shapes=[
            pltpu.VMEM((3, rows, width), deltas.dtype),
            pltpu.VMEM((4, rows // 2, width), deltas.dtype),
            pltpu.VMEM((2, rows // 2, width), jnp.bfloat16),
            pltpu.VMEM((2, rows // 2, width), jnp.bfloat16),
            pltpu.VMEM((layers, 8, 128), jnp.float32),
            pltpu.VMEM((layers, 8, 128), jnp.float32),
            pltpu.VMEM((2, layers, 8, 128), jnp.float32),
            pltpu.VMEM((2, layers, 8, 128), jnp.float32),
            pltpu.VMEM((2, layers, 8, 128), jnp.float32),
            pltpu.VMEM((layers, STEP_ROWS, width), jnp.float32),
            dma((layers * 4 + 2,)),
            dma((4, chunks)),
            dma((4, chunks)),
            dma((2, chunks)),
            dma((2, chunks)),
            dma((2, chunks)),
            dma((2, chunks)),
            dma((2, chunks)),
            dma((2, chunks)),
            dma((2,)),
            dma((2,)),
            dma((2,)),
            dma((2,)),
        ],
        compiler_params=pltpu.CompilerParams(
            collective_id=0, has_side_effects=True, vmem_limit_bytes=kernel_bytes
        ),
        name="outer_step",
    )(
        params.reshape(rows, depth),
        deltas.reshape(rows, depth),
        momentum.reshape(rows, width),
    )
    new_params, new_momentum = pl.pallas_call(
        store_outputs,
        out_shape=(
            jax.ShapeDtypeStruct((rows, depth), params.dtype),
            jax.ShapeDtypeStruct((rows, width), momentum.dtype),
        ),
        in_specs=[vmem] * 2,
        out_specs=(hbm, hbm),
        scratch_shapes=[dma((rep + 1,))],
        compiler_params=pltpu.CompilerParams(vmem_limit_bytes=1 << 20),
        name="store_outputs",
    )(
        pltpu.with_memory_space_constraint(blocks, pltpu.VMEM),
        pltpu.with_memory_space_constraint(fresh_moment, pltpu.VMEM),
    )
    return (
        new_params.reshape(params.shape),
        new_momentum.reshape(momentum.shape),
    )


def solution(mesh):
    placed = (P(None, "fsdp", None), P("rep", None, "fsdp", None), P(None, "fsdp", "rep"))
    return jax.shard_map(
        functools.partial(on_device, mesh.shape["rep"], mesh.shape["fsdp"]),
        mesh=mesh,
        in_specs=placed,
        out_specs=(P(None, "fsdp", None), P(None, "fsdp", "rep")),
        check_vma=False,
    )
```

```python
import functools

import jax
import jax.numpy as jnp
from jax import lax
from jax.experimental import pallas as pl
from jax.experimental.pallas import tpu as pltpu
from jax.sharding import PartitionSpec as P

Q_ROWS = 4096
KV_ROWS = 2048


clip_share = 0.5
peak_eps = 1e-06
outer_rate = 0.7
momentum_decay = 0.9

MESH = pl.DeviceIdType.MESH
CHUNKS_PER_LAYER = 4
EARLY_CHUNKS = 2
STEP_ROWS = 16

Y_OWN, Y_RELAY, X_OWN, X_RELAY = range(4)


def tensor_of(shard, shard_rows):
    row = shard * shard_rows
    return (row >= Q_ROWS).astype(jnp.int32) + (row >= Q_ROWS + KV_ROWS).astype(jnp.int32)


def kernel(
    layers, fsdp, params, deltas, moment, new_params, new_moment,
    local, raw, sum_out, sum_in,
    peak, group_peak, group_peak_in, run_peak, run_peak_in, tau,
    load_sem, raw_send, raw_recv, sum_send, sum_recv,
    own_send, own_recv, relay_send, relay_recv,
    group_send, group_recv, run_send, run_recv,
):
    rows, width = moment.shape
    chunks = layers * CHUNKS_PER_LAYER
    chunk = rows // chunks
    half = chunk // 2
    layer_rows = rows // layers
    me = lax.axis_index("rep")
    shard = lax.axis_index("fsdp")
    y, x = me // 2, me % 2
    over_x = y * 2 + (1 - x)
    over_y = (1 - y) * 2 + x
    diagonal = (1 - y) * 2 + (1 - x)
    blocks = (me, over_x, over_y, diagonal)

    def columns(block):
        return pl.ds(pl.multiple_of(block * width, 128), width)

    def whole(c):
        return pl.ds(pl.multiple_of(c * chunk, STEP_ROWS), chunk)

    def first(c):
        return pl.ds(pl.multiple_of(c * chunk, STEP_ROWS), half)

    def second(c):
        return pl.ds(pl.multiple_of(c * chunk + half, STEP_ROWS), half)

    def packed(c):
        return pl.ds(pl.multiple_of(c * half, STEP_ROWS), half)

    def remote(src, dst, send, recv, axis, target):
        return pltpu.make_async_remote_copy(
            src_ref=src, dst_ref=dst, send_sem=send, recv_sem=recv,
            device_id={axis: target}, device_id_type=MESH,
        )

    loads = []
    for layer in range(layers):
        span = pl.ds(layer * layer_rows, layer_rows)
        for slot, block in enumerate(blocks):
            loads.append(
                pltpu.make_async_copy(
                    deltas.at[span, columns(block)],
                    local.at[slot, span] if slot < 3 else new_params.at[diagonal, span],
                    load_sem.at[layer * 4 + slot],
                )
            )
    load_params = pltpu.make_async_copy(params.at[:, columns(me)], new_params.at[me], load_sem.at[layers * 4])
    load_moment = pltpu.make_async_copy(moment, new_moment, load_sem.at[layers * 4 + 1])
    for load in loads:
        load.start()

    barrier = pltpu.get_barrier_semaphore()
    for target in (over_x, over_y):
        pl.semaphore_signal(barrier, inc=1, device_id={"rep": target}, device_id_type=MESH)

    @pl.when(shard > 0)
    def _():
        pl.semaphore_signal(barrier, inc=1, device_id={"fsdp": shard - 1}, device_id_type=MESH)

    @pl.when(shard < fsdp - 1)
    def _():
        pl.semaphore_signal(barrier, inc=1, device_id={"fsdp": shard + 1}, device_id_type=MESH)

    inner = jnp.where(shard > 0, 1, 0) + jnp.where(shard < fsdp - 1, 1, 0)
    pl.semaphore_wait(barrier, 2 + inner)

    def raw_copy(kind, c):
        target = over_y if kind in (Y_OWN, Y_RELAY) else over_x
        span = first(c) if kind in (Y_OWN, Y_RELAY) else second(c)
        block = diagonal if kind in (Y_RELAY, X_RELAY) else target
        return remote(
            deltas.at[span, columns(block)], raw.at[kind, packed(c)],
            raw_send.at[kind, c], raw_recv.at[kind, c], "rep", target,
        )

    def sum_copy(link, c):
        return remote(
            sum_out.at[link, packed(c)], sum_in.at[link, packed(c)],
            sum_send.at[link, c], sum_recv.at[link, c], "rep", over_x if link == 0 else over_y,
        )

    def own_copy(link, c):
        return remote(
            new_params.at[me, whole(c)], new_params.at[me, whole(c)],
            own_send.at[link, c], own_recv.at[link, c], "rep", over_x if link == 0 else over_y,
        )

    def relay_copy(link, c):
        piece = (over_y, second(c)) if link == 0 else (over_x, first(c))
        return remote(
            new_params.at[piece], new_params.at[piece],
            relay_send.at[link, c], relay_recv.at[link, c], "rep", over_x if link == 0 else over_y,
        )

    def start_raw(c, carry):
        for kind in (Y_RELAY, X_RELAY, Y_OWN, X_OWN):
            raw_copy(kind, c).start()
        return carry

    lax.fori_loop(0, EARLY_CHUNKS, start_raw, 0)

    for layer in range(layers):
        for slot in range(4):
            loads[layer * 4 + slot].wait()

        def largest(i, top):
            span = pl.ds(pl.multiple_of(layer * layer_rows + i * STEP_ROWS, STEP_ROWS), STEP_ROWS)
            for slot in range(3):
                top = jnp.maximum(top, jnp.abs(local[slot, span, :]))
            return jnp.maximum(top, jnp.abs(new_params[diagonal, span, :]))

        top = lax.fori_loop(
            0, layer_rows // STEP_ROWS, largest, jnp.zeros((STEP_ROWS, width), local.dtype)
        ).astype(jnp.float32)
        top = functools.reduce(
            jnp.maximum, [top[:, k * 128 : (k + 1) * 128] for k in range(width // 128)]
        )
        peak[layer] = jnp.maximum(top[:8], top[8:])

    load_params.start()
    load_moment.start()

    def group_copy(step):
        return remote(
            peak if step == 0 else group_peak, group_peak_in.at[step],
            group_send.at[step], group_recv.at[step], "rep", over_x if step == 0 else over_y,
        )

    group_copy(0).start()
    lax.fori_loop(EARLY_CHUNKS, EARLY_CHUNKS + 1, start_raw, 0)
    group_copy(0).wait_recv()
    group_peak[...] = jnp.maximum(peak[...], group_peak_in[0])
    group_copy(1).start()
    lax.fori_loop(EARLY_CHUNKS + 1, chunks, start_raw, 0)
    group_copy(1).wait_recv()
    for way in range(2):
        run_peak[way] = jnp.maximum(group_peak[...], group_peak_in[1])

    def line_copy(way):
        return remote(
            run_peak.at[way], run_peak_in.at[way], run_send.at[way], run_recv.at[way],
            "fsdp", shard + 1 if way == 0 else shard - 1,
        )

    mine = tensor_of(shard, layer_rows)
    has_left, has_right = shard > 0, shard < fsdp - 1
    for way, behind, ahead, before in (
        (0, has_left, has_right, shard - 1),
        (1, has_right, has_left, shard + 1),
    ):
        share = jnp.where(tensor_of(before, layer_rows) == mine, jnp.float32(1.0), jnp.float32(0.0))

        @pl.when(behind)
        def _():
            line_copy(way).wait_recv()
            run_peak[way] = jnp.maximum(run_peak[way], run_peak_in[way] * share)

        @pl.when(ahead)
        def _():
            line_copy(way).start()

    for layer in range(layers):
        top = jnp.maximum(run_peak[0, layer], run_peak[1, layer])
        top = jnp.max(jnp.max(top, axis=0, keepdims=True), axis=1, keepdims=True)
        tau[layer] = jnp.broadcast_to(clip_share * (top + peak_eps), tau.shape[1:])

    def code(values, scale):
        return jnp.clip(values.astype(jnp.float32) / scale, -1.0, 1.0).astype(jnp.bfloat16).astype(jnp.float32)

    def relay_sums(c, carry):
        layer = c // CHUNKS_PER_LAYER
        for link, kind in ((0, Y_RELAY), (1, X_RELAY)):
            raw_copy(kind, c).wait_recv()
            start = c * chunk + link * half

            def add(i, inner):
                here = pl.ds(pl.multiple_of(start + i * STEP_ROWS, STEP_ROWS), STEP_ROWS)
                there = pl.ds(pl.multiple_of(c * half + i * STEP_ROWS, STEP_ROWS), STEP_ROWS)
                scale = tau[layer]
                total = code(local[1 + link, here, :], scale) + code(raw[kind, there, :], scale)
                sum_out[link, there, :] = total.astype(jnp.bfloat16)
                return inner

            lax.fori_loop(0, half // STEP_ROWS, add, 0)
            sum_copy(link, c).start()
        return carry

    lax.fori_loop(0, chunks, relay_sums, 0)

    load_params.wait()
    load_moment.wait()

    def update(c, carry):
        layer = c // CHUNKS_PER_LAYER
        for link, kind in ((0, Y_OWN), (1, X_OWN)):
            raw_copy(kind, c).wait_recv()
            sum_copy(link, c).wait_recv()
            start = c * chunk + link * half

            def apply(i, inner):
                here = pl.ds(pl.multiple_of(start + i * STEP_ROWS, STEP_ROWS), STEP_ROWS)
                there = pl.ds(pl.multiple_of(c * half + i * STEP_ROWS, STEP_ROWS), STEP_ROWS)
                scale = tau[layer]
                total = code(local[0, here, :], scale) + code(raw[kind, there, :], scale)
                total = total + sum_in[link, there, :].astype(jnp.float32)
                outer = scale * total / jnp.float32(4)
                moved = momentum_decay * new_moment[here, :] + outer
                new_moment[here, :] = moved
                new_params[me, here, :] = (
                    new_params[me, here, :].astype(jnp.float32) - outer_rate * (outer + momentum_decay * moved)
                ).astype(jnp.bfloat16)
                return inner

            lax.fori_loop(0, half // STEP_ROWS, apply, 0)
        own_copy(0, c).start()
        own_copy(1, c).start()
        return carry

    lax.fori_loop(0, chunks, update, 0)

    def relay(c, carry):
        for link in range(2):
            own_copy(link, c).wait_recv()

            @pl.when(c < chunks - 1)
            def _():
                relay_copy(1 - link, c).start()

        return carry

    lax.fori_loop(0, chunks, relay, 0)

    def drain(c, carry):
        for kind in range(4):
            raw_copy(kind, c).wait_send()
        for link in range(2):
            sum_copy(link, c).wait_send()
            own_copy(link, c).wait_send()

            @pl.when(c < chunks - 1)
            def _():
                relay_copy(link, c).wait()

        return carry

    for way, ahead in ((0, has_right), (1, has_left)):

        @pl.when(ahead)
        def _():
            line_copy(way).wait_send()

    for step in range(2):
        group_copy(step).wait_send()
    lax.fori_loop(0, chunks, drain, 0)


def store_outputs(blocks, fresh_moment, new_params, new_moment, sems):
    count, _, width = blocks.shape
    stores = [
        pltpu.make_async_copy(blocks.at[k], new_params.at[:, pl.ds(k * width, width)], sems.at[k])
        for k in range(count)
    ]
    stores.append(pltpu.make_async_copy(fresh_moment, new_moment, sems.at[count]))
    for store in stores:
        store.start()
    for store in stores:
        store.wait()


def store_tail(piece_y, piece_x, _, new_params, staged, sems):
    rows = new_params.shape[0]
    half, width = piece_y.shape
    me = lax.axis_index("rep")
    diagonal = 3 - me
    columns = pl.ds(pl.multiple_of(diagonal * width, 128), width)
    loads = [
        pltpu.make_async_copy(piece, staged.at[k], sems.at[k]) for k, piece in enumerate((piece_y, piece_x))
    ]
    stores = [
        pltpu.make_async_copy(
            staged.at[k], new_params.at[pl.ds(rows - (2 - k) * half, half), columns], sems.at[2 + k]
        )
        for k in range(2)
    ]
    for load in loads:
        load.start()
    for load, store in zip(loads, stores):
        load.wait()
        store.start()
    for store in stores:
        store.wait()


def on_device(rep, fsdp, params, deltas, momentum):
    layers, shard_rows, depth = params.shape
    width = momentum.shape[2]
    rows = layers * shard_rows
    chunks = layers * CHUNKS_PER_LAYER
    assert rep == 4 and width * rep == depth and width % 128 == 0
    assert Q_ROWS % shard_rows == 0 and KV_ROWS % shard_rows == 0
    assert shard_rows % (CHUNKS_PER_LAYER * 2 * STEP_ROWS) == 0
    block_bytes = rows * width * 2
    kernel_bytes = block_bytes * 7 + (2 << 20)
    dma = pltpu.SemaphoreType.DMA
    hbm = pl.BlockSpec(memory_space=pl.ANY)
    vmem = pl.BlockSpec(memory_space=pltpu.VMEM)
    blocks, fresh_moment = pl.pallas_call(
        functools.partial(kernel, layers, fsdp),
        out_shape=(
            pltpu.VMEM((rep, rows, width), params.dtype),
            pltpu.VMEM((rows, width), momentum.dtype),
        ),
        in_specs=[hbm] * 3,
        out_specs=(vmem, vmem),
        scratch_shapes=[
            pltpu.VMEM((3, rows, width), deltas.dtype),
            pltpu.VMEM((4, rows // 2, width), deltas.dtype),
            pltpu.VMEM((2, rows // 2, width), jnp.bfloat16),
            pltpu.VMEM((2, rows // 2, width), jnp.bfloat16),
            pltpu.VMEM((layers, 8, 128), jnp.float32),
            pltpu.VMEM((layers, 8, 128), jnp.float32),
            pltpu.VMEM((2, layers, 8, 128), jnp.float32),
            pltpu.VMEM((2, layers, 8, 128), jnp.float32),
            pltpu.VMEM((2, layers, 8, 128), jnp.float32),
            pltpu.VMEM((layers, STEP_ROWS, width), jnp.float32),
            dma((layers * 4 + 2,)),
            dma((4, chunks)),
            dma((4, chunks)),
            dma((2, chunks)),
            dma((2, chunks)),
            dma((2, chunks)),
            dma((2, chunks)),
            dma((2, chunks)),
            dma((2, chunks)),
            dma((2,)),
            dma((2,)),
            dma((2,)),
            dma((2,)),
        ],
        compiler_params=pltpu.CompilerParams(
            collective_id=0, has_side_effects=True, vmem_limit_bytes=kernel_bytes
        ),
        name="outer_step",
    )(
        params.reshape(rows, depth),
        deltas.reshape(rows, depth),
        momentum.reshape(rows, width),
    )
    half = rows // chunks // 2
    me = lax.axis_index("rep")
    over_x = me // 2 * 2 + 1 - me % 2
    over_y = (1 - me // 2) * 2 + me % 2
    tail = rows - 2 * half
    piece_y = lax.dynamic_slice(blocks, (over_x, tail, 0), (1, half, width))[0]
    piece_x = lax.dynamic_slice(blocks, (over_y, tail + half, 0), (1, half, width))[0]
    piece_y = lax.ppermute(piece_y, "rep", [(k, (k + 2) % 4) for k in range(4)])
    piece_x = lax.ppermute(piece_x, "rep", [(k, k + 1 - 2 * (k % 2)) for k in range(4)])
    new_params, new_momentum = pl.pallas_call(
        store_outputs,
        out_shape=(
            jax.ShapeDtypeStruct((rows, depth), params.dtype),
            jax.ShapeDtypeStruct((rows, width), momentum.dtype),
        ),
        in_specs=[vmem] * 2,
        out_specs=(hbm, hbm),
        scratch_shapes=[dma((rep + 1,))],
        compiler_params=pltpu.CompilerParams(vmem_limit_bytes=1 << 20),
        cost_estimate=pl.CostEstimate(flops=0, bytes_accessed=rows * depth * 4, transcendentals=0),
        name="store_outputs",
    )(
        pltpu.with_memory_space_constraint(blocks, pltpu.VMEM),
        pltpu.with_memory_space_constraint(fresh_moment, pltpu.VMEM),
    )
    new_params = pl.pallas_call(
        store_tail,
        out_shape=jax.ShapeDtypeStruct((rows, depth), params.dtype),
        in_specs=[hbm] * 3,
        out_specs=hbm,
        input_output_aliases={2: 0},
        scratch_shapes=[pltpu.VMEM((2, half, width), params.dtype), dma((4,))],
        compiler_params=pltpu.CompilerParams(vmem_limit_bytes=4 << 20),
        name="store_tail",
    )(piece_y, piece_x, new_params)
    return (
        new_params.reshape(params.shape),
        new_momentum.reshape(momentum.shape),
    )


def solution(mesh):
    placed = (P(None, "fsdp", None), P("rep", None, "fsdp", None), P(None, "fsdp", "rep"))
    return jax.shard_map(
        functools.partial(on_device, mesh.shape["rep"], mesh.shape["fsdp"]),
        mesh=mesh,
        in_specs=placed,
        out_specs=(P(None, "fsdp", None), P(None, "fsdp", "rep")),
        check_vma=False,
    )
```
